512 devices in a mesh: leaf: 128 (over z, y, core), rep: 4 (over x).
Axes of the slice: x: 4, y: 4, z: 16, core: 2. Of those that a mesh axis runs over, the one named last changes fastest.
Arguments:
- positions: float32 [3, 8192, 128], P(None, ('leaf', 'rep')), may hold values from -6 to 6
- density: float32 [3, 8192, 128], P(None, ('leaf', 'rep')), may hold values from -6 to 6
- near_offset: int32 [8192, 12], P(('leaf', 'rep')), may hold values from -2 to 2
- near_count: int32 [8192], P(('leaf', 'rep')), may hold values from 1 to 12
- inter_list: int32 [512, 189], P(('leaf', 'rep')), may hold values from 0 to 511
- operator_index: int32 [512, 189], P(('leaf', 'rep')), may hold values from 0 to 3
- lattice_index: int32 [512], P(('leaf', 'rep')), may hold values from 0 to 1
- up_weight: bfloat16 [512, 384], replicated, may hold values from -0.3125 to 0.3125
- m2l_operators: bfloat16 [4, 512, 512], replicated, may hold values from -0.0390625 to 0.0390625
- lattice_operators: bfloat16 [2, 512, 512], replicated, may hold values from -0.01171875 to 0.01171875
- down_weight: bfloat16 [384, 512], replicated, may hold values from -0.5 to 0.5
Outputs:
- velocity: float32 [3, 8192, 128], P(None, ('leaf', 'rep'))
The draws below stay inside these ranges and needn't reach their ends.
Inputs may be any that keep to these rules, and one draw needn't show every extreme that they name: `near_offset`: leaf g's near source leaves are (g + offset) mod 8192; slots at or past near_count are unused.
All inputs are finite; a program needn't handle non-finite values.
Results may differ from the reference program's by a relative error of at most 0.02.
Values may be sent and summed in bfloat16 or wider, within the bound.
A program may use at most 64 MiB of HBM per device.

```python
import math
import jax
import jax.numpy as jnp
from jax import lax

NODES = 128
COEF = 512
LEAF_DEV = 16
SPAN = 2
NEAR_MAX = 12
NIL = 189
NOP = 4
NLAT = 2
BOXES = 512
LEAVES = 8192


def place_ends(values, own_key, low, largest):
    spot = [jax.random.randint(jax.random.fold_in(own_key, axis), (), 0, length) for axis, length in enumerate(values.shape)]
    widest = values.shape.index(max(values.shape))
    next_to = spot[:widest] + [(spot[widest] + 1) % values.shape[widest]] + spot[widest + 1:]
    return values.at[tuple(spot)].set(low).at[tuple(next_to)].set(largest)


def steps_of(rng, shape, shards, low, high):
    loudness = 1.0
    for axis_at, shards_of in shards:
        draws = jax.random.uniform(jax.random.fold_in(jax.random.fold_in(rng, 6), axis_at), (shards_of,), jnp.float32, low / len(shards), high / len(shards))
        loudness = loudness * jnp.repeat(jnp.exp(draws), shape[axis_at] // shards_of).reshape((-1,) + (1,) * (len(shape) - 1 - axis_at))
    return loudness


def noise(key, shape, width, reach, split=(), kind=jnp.bfloat16):
    gain = steps_of(key, shape, split, -0.22, 0.18) if split else 1.0
    drawn = jax.random.normal(key, shape, jnp.float32) * width * gain
    return jnp.minimum(jnp.maximum(drawn, -reach), reach).astype(kind)


def setup_inputs(seed: int = 0) -> dict:
    arg_keys = jax.random.split(jax.random.key(seed), 12)
    return {
        "positions": noise(arg_keys[0], (3, LEAVES, NODES), 1.0, 6.0, ((1, 512),), jnp.float32),
        "density": noise(arg_keys[1], (3, LEAVES, NODES), 1.0, 6.0, ((1, 512),), jnp.float32),
        "near_offset": place_ends(jax.random.randint(arg_keys[2], (LEAVES, NEAR_MAX), 0 - SPAN, SPAN + 1), jax.random.fold_in(arg_keys[2], 1), 0 - SPAN, SPAN).astype(jnp.int32),
        "near_count": place_ends(jax.random.randint(arg_keys[3], (LEAVES,), 1, NEAR_MAX + 1), jax.random.fold_in(arg_keys[3], 1), 1, NEAR_MAX).astype(jnp.int32),
        "inter_list": place_ends(jax.random.randint(arg_keys[4], (BOXES, NIL), 0, BOXES), jax.random.fold_in(arg_keys[4], 1), 0, BOXES - 1).astype(jnp.int32),
        "operator_index": place_ends(jax.random.randint(arg_keys[5], (BOXES, NIL), 0, NOP), jax.random.fold_in(arg_keys[5], 1), 0, NOP - 1).astype(jnp.int32),
        "lattice_index": place_ends(jax.random.randint(arg_keys[6], (BOXES,), 0, NLAT), jax.random.fold_in(arg_keys[6], 1), 0, NLAT - 1).astype(jnp.int32),
        "up_weight": noise(arg_keys[7], (COEF, 3 * NODES), (3 * NODES) ** -0.5, 0.3125),
        "m2l_operators": noise(arg_keys[8], (NOP, COEF, COEF), (COEF * NIL // NOP) ** -0.5, 0.0390625),
        "lattice_operators": noise(arg_keys[9], (NLAT, COEF, COEF), (COEF * BOXES) ** -0.5, 0.01171875),
        "down_weight": noise(arg_keys[10], (3 * NODES, COEF), (COEF // 4) ** -0.5, 0.5),
    }


def stokes_tile(target, source_pos, source_force, live_slots):
    offsets_xyz = target[:, None, :, None] - source_pos[:, :, None, :]
    distance_sq = lax.optimization_barrier(jnp.sum(offsets_xyz * offsets_xyz, axis=0)) + 0.05
    inverse = lax.rsqrt(distance_sq)
    inverse_cube = inverse * inverse * inverse
    projected = lax.optimization_barrier(jnp.sum(offsets_xyz * source_force[:, :, None, :], axis=0))
    kernel_terms = source_force[:, :, None, :] * inverse + offsets_xyz * (projected * inverse_cube)
    kernel_terms = kernel_terms * live_slots[None, :, None, None]
    return lax.optimization_barrier(jnp.sum(kernel_terms, axis=(1, 3))) * (1.0 / (8.0 * math.pi))

def reference(positions, density, near_offset, near_count, inter_list, operator_index, lattice_index, up_weight, m2l_operators, lattice_operators, down_weight):
    slot_range = jnp.arange(NEAR_MAX, dtype=jnp.int32)

    def one_leaf(leaf_slot):
        target = positions[:, leaf_slot]
        source_ids = ((leaf_slot + near_offset[leaf_slot]) % LEAVES).astype(jnp.int32)
        source_pos = jnp.take(positions, source_ids, axis=1)
        source_force = jnp.take(density, source_ids, axis=1)
        live_slots = (slot_range < near_count[leaf_slot]).astype(jnp.float32)
        return stokes_tile(target, source_pos, source_force, live_slots)
    near_part = lax.map(one_leaf, jnp.arange(LEAVES, dtype=jnp.int32))
    near_part = jnp.transpose(near_part, (1, 0, 2))
    damping = 1.0 / (1.0 + lax.optimization_barrier(jnp.sum(positions * positions, axis=0)))
    weighted = (density * damping[None]).reshape(3, BOXES, LEAF_DEV, NODES).sum(axis=2)
    summed = jnp.transpose(weighted, (1, 0, 2)).reshape(BOXES, 3 * NODES).astype(jnp.bfloat16)
    coarse = jnp.dot(summed, up_weight.T, preferred_element_type=jnp.float32).astype(jnp.bfloat16)
    total = lax.optimization_barrier(jnp.sum(coarse.astype(jnp.float32), axis=0)).astype(jnp.bfloat16)
    kind_range = jnp.arange(NOP, dtype=jnp.int32)

    def one_box(box_args):
        box_ids, op_kinds, lattice_kind = box_args
        chosen = jnp.take(coarse, box_ids, axis=0).astype(jnp.float32)
        selector = (op_kinds[None, :] == kind_range[:, None]).astype(jnp.float32)
        grouped = jnp.dot(selector, chosen, precision=lax.Precision.HIGHEST).astype(jnp.bfloat16)
        local = jnp.einsum('tij,tj->i', m2l_operators.astype(jnp.float32), grouped.astype(jnp.float32), precision=lax.Precision.HIGHEST)
        local = local + jnp.dot(lattice_operators[lattice_kind], total, preferred_element_type=jnp.float32)
        local_bf = local.astype(jnp.bfloat16)
        return jnp.dot(down_weight, local_bf, preferred_element_type=jnp.float32).reshape(3, NODES)
    far_part = lax.map(one_box, (inter_list, operator_index, lattice_index))
    far_leaves = jnp.repeat(jnp.transpose(far_part, (1, 0, 2)), LEAF_DEV, axis=1)
    return near_part + damping[None] * far_leaves
```

```python
import functools
import math

import jax
import jax.numpy as jnp
from jax import lax
from jax.experimental import pallas as pl
from jax.experimental.pallas import tpu as pltpu
from jax.sharding import PartitionSpec as P

MESH = pl.DeviceIdType.MESH
F32 = jnp.float32
BF16 = jnp.bfloat16
NT = (((1,), (1,)), ((), ()))


def dot_nt(a, b):
    return lax.dot_general(a, b, NT, preferred_element_type=F32)


def split3(v):
    hi = v.astype(BF16).astype(F32)
    rest = v - hi
    mid = rest.astype(BF16).astype(F32)
    return hi, mid, rest - mid


def kernel(
    dims,
    early,
    middle,
    pos_ref,
    den_ref,
    off_ref,
    cnt_ref,
    ids_ref,
    ops_ref,
    lat_idx_ref,
    up_hbm,
    m2l_hbm,
    lat_hbm,
    down_hbm,
    out_ref,
    up_v,
    m2l_v,
    lat_v,
    down_v,
    halo,
    id_s,
    op_s,
    csend,
    crecv,
    gz,
    stage,
    plane,
    psend,
    precv,
    b_s,
    a_s,
    l_s,
    at_s,
    m_s,
    acc_s,
    wsem,
    zsend,
    zrecv,
    xsend,
    xrecv,
    hsend,
    hrecv,
    osend,
    orecv,
):
    nz, ny, nx = dims
    planes = ny * nx
    per_z = 2 * ny
    leaf = lax.axis_index("leaf")
    rep = lax.axis_index("rep")
    z = leaf // per_z
    y = lax.rem(leaf // 2, ny)
    core = lax.rem(leaf, 2)
    box = leaf * nx + rep
    boxes = nz * ny * nx * 2
    me_p = y * nx + rep

    def z_peer(d):
        return (lax.rem(z + d, nz) * per_z + y * 2 + core, rep)

    def p_peer(d):
        return (
            z * per_z + lax.rem(y + d // nx, ny) * 2 + core,
            lax.rem(rep + lax.rem(d, nx), nx),
        )

    partner = (leaf + 1 - 2 * core, rep)
    after = lax.rem(box + 1, boxes)
    before = lax.rem(box + boxes - 1, boxes)
    after = (after // nx, lax.rem(after, nx))
    before = (before // nx, lax.rem(before, nx))

    loads = [
        pltpu.make_async_copy(src, dst, wsem.at[i])
        for i, (src, dst) in enumerate(
            [(up_hbm, up_v), (m2l_hbm, m2l_v), (lat_hbm, lat_v), (down_hbm, down_v)]
        )
    ]
    for load in loads:
        load.start()

    barrier = pltpu.get_barrier_semaphore()

    def greet(peer):
        pl.semaphore_signal(barrier, inc=1, device_id=peer, device_id_type=MESH)

    @pl.loop(1, nz)
    def _(d):
        greet(z_peer(d))

    @pl.loop(1, planes)
    def _(d):
        greet(p_peer(d))

    greet(partner)
    greet(after)
    greet(before)

    x = [pos_ref[c] for c in range(3)]
    f = [den_ref[c] for c in range(3)]
    x2 = x[0] * x[0] + x[1] * x[1] + x[2] * x[2]
    damping = 1.0 / (1.0 + x2)
    summed = jnp.concatenate(
        [jnp.sum(f[c] * damping, axis=0, keepdims=True) for c in range(3)], axis=1
    )
    summed = jnp.broadcast_to(summed, (8, summed.shape[1])).astype(BF16)
    loads[0].wait()
    coarse = dot_nt(summed, up_v[...]).astype(BF16).astype(F32)
    gz[z] = coarse[0:1]

    half = boxes // 2
    id_s[...] = jnp.full(id_s.shape, -1, jnp.int32)
    op_s[...] = jnp.full(op_s.shape, -1, jnp.int32)
    nil = ids_ref.shape[1]
    id_s[0:1, 0:nil] = ids_ref[...]
    op_s[0:1, 0:nil] = ops_ref[...]
    ids = id_s[0:1, :]
    kinds = op_s[0:1, :]
    sx, sy = nx.bit_length() - 1, ny.bit_length() - 1
    id_x = ids & (nx - 1)
    id_core = (ids >> sx) & 1
    id_y = (ids >> (sx + 1)) & (ny - 1)
    id_z = ids >> (sx + 1 + sy)
    column = jnp.where(ids < 0, -1, id_core * half + (id_y * nx + id_x) * nz + id_z)
    width = ids.shape[1]
    rows = lax.broadcasted_iota(jnp.int32, (boxes, width), 0)
    hot = jnp.where(rows == column, 1.0, 0.0).astype(BF16)
    kind_rows = lax.broadcasted_iota(jnp.int32, (8, width), 0)
    picks = jnp.where(kind_rows == kinds, 1.0, 0.0).astype(BF16)
    counts = dot_nt(picks, hot)
    one_row = lax.broadcasted_iota(jnp.int32, counts.shape, 0) == 4
    counts = jnp.where(one_row, 1.0, counts)
    left, right = counts[:, :half], counts[:, half:]
    first = core == 0
    csend[...] = jnp.where(first, right, left)
    own_counts = jnp.where(first, left, right)

    leaves = x2.shape[0]
    leaf_rows = lax.broadcasted_iota(jnp.int32, off_ref.shape, 0)
    slots = lax.broadcasted_iota(jnp.int32, off_ref.shape, 1)
    used = jnp.zeros(off_ref.shape, jnp.int32)
    for g in range(leaves):
        used = jnp.where(leaf_rows == g, cnt_ref[g], used)
    for o in range(5):
        hit = jnp.where((off_ref[...] == o - 2) & (slots < used), 1.0, 0.0)
        m_s[o] = jnp.broadcast_to(jnp.sum(hit, axis=1, keepdims=True), x2.shape)

    ones = jnp.ones(x2.shape, F32)
    zeros = jnp.zeros(x2.shape, F32)
    parts = [split3(v) for v in x]
    for s in range(3):
        for c in range(3):
            b_s[:, 3 * s + c, :] = parts[c][s]
    for s, v in enumerate(split3(x2 + 0.05)):
        b_s[:, 9 + s, :] = v
        b_s[:, 12 + s, :] = ones
    b_s[:, 15, :] = zeros

    def source_rows(lo, sx_, sf_):
        n = sx_[0].shape[0]
        at = pl.ds(lo, n)
        one, zero = jnp.ones(sx_[0].shape, F32), jnp.zeros(sx_[0].shape, F32)
        yy = [v.astype(BF16).astype(F32) for v in sx_]
        ff = [v.astype(BF16).astype(F32) for v in sf_]
        y2 = split3(yy[0] * yy[0] + yy[1] * yy[1] + yy[2] * yy[2])
        yf = split3(-(yy[0] * ff[0] + yy[1] * ff[1] + yy[2] * ff[2]))
        for s in range(3):
            for c in range(3):
                a_s[at, 3 * s + c, 0:128] = -2.0 * yy[c]
                a_s[at, 3 * s + c, 128:256] = ff[c]
            a_s[at, 9 + s, 0:128] = one
            a_s[at, 9 + s, 128:256] = zero
            a_s[at, 12 + s, 0:128] = y2[s]
            a_s[at, 12 + s, 128:256] = yf[s]
            l_s[at, s, 0:128] = ff[s]
            l_s[at, s, 128:256] = -yy[s]
        a_s[at, 15, 0:128] = zero
        a_s[at, 15, 128:256] = zero
        l_s[at, 3, 0:128] = zero
        l_s[at, 3, 128:256] = one
        for r in range(4, 8):
            l_s[at, r, 0:128] = zero
            l_s[at, r, 128:256] = zero

    def turn(lo, hi):
        @pl.loop(lo, hi)
        def _(i):
            at_s[i] = a_s[i].T.astype(BF16)

    source_rows(2, x, f)
    turn(2, leaves + 2)

    def near(lo, hi):
        @pl.loop(lo, hi)
        def _(g):
            target = b_s[g].astype(BF16)
            total = jnp.zeros((8, 128), F32)
            for o in range(5):
                qp = jnp.dot(at_s[g + o], target, preferred_element_type=F32)
                inv = lax.rsqrt(qp[0:128])
                w = qp[128:256] * (inv * inv * inv)
                pair = jnp.concatenate([inv, w], axis=0).astype(BF16)
                r = jnp.dot(l_s[g + o].astype(BF16), pair, preferred_element_type=F32)
                total = total + r * m_s[o, pl.ds(g, 1), :]
            acc_s[g] = total

    near(2, early)

    pl.semaphore_wait(barrier, nz + planes + 1)

    def z_copy(d):
        return pltpu.make_async_remote_copy(
            src_ref=gz.at[z],
            dst_ref=gz.at[z],
            send_sem=zsend.at[d],
            recv_sem=zrecv.at[d],
            device_id=z_peer(d),
            device_id_type=MESH,
        )

    def p_copy(d):
        return pltpu.make_async_remote_copy(
            src_ref=plane.at[me_p],
            dst_ref=plane.at[me_p],
            send_sem=xsend.at[d],
            recv_sem=xrecv.at[d],
            device_id=p_peer(d),
            device_id_type=MESH,
        )

    @pl.loop(1, nz)
    def _(d):
        z_copy(d).start()

    def remote(src, dst, s, r, peer):
        return pltpu.make_async_remote_copy(
            src_ref=src, dst_ref=dst, send_sem=s, recv_sem=r, device_id=peer, device_id_type=MESH
        )

    high = pl.ds(leaves - 8, 8)
    halos = [
        remote(pos_ref.at[:, high, :], halo.at[0], hsend.at[0], hrecv.at[0], after),
        remote(den_ref.at[:, high, :], halo.at[1], hsend.at[1], hrecv.at[1], after),
        remote(pos_ref.at[:, 0:8, :], halo.at[2], hsend.at[2], hrecv.at[2], before),
        remote(den_ref.at[:, 0:8, :], halo.at[3], hsend.at[3], hrecv.at[3], before),
    ]
    for copy in halos:
        copy.start()
    share = remote(csend, crecv, osend.at[0], orecv.at[0], partner)
    share.start()

    near(early, middle)

    @pl.loop(1, nz)
    def _(d):
        z_copy(d).wait_recv()

    for i in range(nz):
        stage[i : i + 1, :] = gz[i]
    plane[me_p] = stage[...].astype(BF16)

    @pl.loop(1, planes)
    def _(d):
        p_copy(d).start()

    near(middle, leaves - 2)
    for copy in halos:
        copy.wait_recv()
    source_rows(0, [halo[0, c, 6:8, :] for c in range(3)], [halo[1, c, 6:8, :] for c in range(3)])
    source_rows(
        leaves + 2, [halo[2, c, 0:2, :] for c in range(3)], [halo[3, c, 0:2, :] for c in range(3)]
    )
    turn(0, 2)
    turn(leaves + 2, leaves + 4)
    near(0, 2)
    near(leaves - 2, leaves)

    scale = 1.0 / (8.0 * math.pi)
    lever = acc_s[:, 3, :]
    near_part = [(acc_s[:, c, :] + x[c] * lever) * scale for c in range(3)]

    share.wait_recv()
    selector = jnp.concatenate([own_counts, crecv[...]], axis=0).astype(BF16)
    for load in loads[1:]:
        load.wait()

    @pl.loop(1, planes)
    def _(d):
        p_copy(d).wait_recv()

    blocks = plane[...].reshape(half, plane.shape[2])
    partial = jnp.dot(selector, blocks, preferred_element_type=F32)
    psend[...] = partial[8:16]
    swap = remote(psend, precv, osend.at[1], orecv.at[1], partner)
    swap.start()
    swap.wait_recv()
    grouped = (partial[0:8] + precv[...]).astype(BF16)

    def spread(t):
        return jnp.broadcast_to(grouped[t : t + 1].astype(F32), grouped.shape)

    lat_idx = lat_idx_ref[0]
    total = spread(4)
    local = jnp.zeros(grouped.shape, F32)
    for t in range(4):
        local = local + dot_nt(spread(t).astype(BF16), m2l_v[t])
    for i in range(2):
        kept = jnp.where(lat_idx == i, total, 0.0).astype(BF16)
        local = local + dot_nt(kept, lat_v[i])
    far = dot_nt(local.astype(BF16), down_v[...])
    for c in range(3):
        out_ref[c] = near_part[c] + damping * far[0:1, 128 * c : 128 * (c + 1)]

    @pl.loop(1, nz)
    def _(d):
        z_copy(d).wait_send()

    @pl.loop(1, planes)
    def _(d):
        p_copy(d).wait_send()

    for copy in halos + [share, swap]:
        copy.wait_send()


def body(dims, early, middle, pos, den, off, cnt, ids, ops, lat_idx, up, m2l, lat, down):
    nz, ny, nx = dims
    planes = ny * nx
    boxes = nz * planes * 2
    leaves = pos.shape[1]
    coef = up.shape[0]
    vm = pl.BlockSpec(memory_space=pltpu.VMEM)
    sm = pl.BlockSpec(memory_space=pltpu.SMEM)
    hbm = pl.BlockSpec(memory_space=pl.ANY)
    dma = pltpu.SemaphoreType.DMA
    return pl.pallas_call(
        functools.partial(kernel, dims, early, middle),
        out_shape=jax.ShapeDtypeStruct(pos.shape, F32),
        in_specs=[vm, vm, vm, sm, vm, vm, sm, hbm, hbm, hbm, hbm],
        out_specs=vm,
        scratch_shapes=[
            pltpu.VMEM(up.shape, BF16),
            pltpu.VMEM(m2l.shape, BF16),
            pltpu.VMEM(lat.shape, BF16),
            pltpu.VMEM(down.shape, BF16),
            pltpu.VMEM((4, 3, 8, 128), F32),
            pltpu.VMEM((8, 256), jnp.int32),
            pltpu.VMEM((8, 256), jnp.int32),
            pltpu.VMEM((8, boxes // 2), F32),
            pltpu.VMEM((8, boxes // 2), F32),
            pltpu.VMEM((nz, 1, coef), F32),
            pltpu.VMEM((nz, coef), F32),
            pltpu.VMEM((planes, nz, coef), BF16),
            pltpu.VMEM((8, coef), F32),
            pltpu.VMEM((8, coef), F32),
            pltpu.VMEM((leaves, 16, 128), F32),
            pltpu.VMEM((leaves + 4, 16, 256), F32),
            pltpu.VMEM((leaves + 4, 8, 256), F32),
            pltpu.VMEM((leaves + 4, 256, 16), BF16),
            pltpu.VMEM((5, leaves, 128), F32),
            pltpu.VMEM((leaves, 8, 128), F32),
            dma((4,)),
            dma((nz,)),
            dma((nz,)),
            dma((planes,)),
            dma((planes,)),
            dma((4,)),
            dma((4,)),
            dma((2,)),
            dma((2,)),
        ],
        compiler_params=pltpu.CompilerParams(
            collective_id=0, has_side_effects=True, vmem_limit_bytes=32 * 1024 * 1024
        ),
        name="fmm",
    )(pos, den, off, cnt, ids, ops, lat_idx, up, m2l, lat, down)


def solution(mesh):
    sizes = dict(mesh.shape)
    nx = sizes["rep"]
    ny = 4
    nz = sizes["leaf"] // (2 * ny)
    both = ("leaf", "rep")
    in_specs = (
        P(None, both, None),
        P(None, both, None),
        P(both, None),
        P(both),
        P(both, None),
        P(both, None),
        P(both),
        P(),
        P(),
        P(),
        P(),
    )
    run = functools.partial(body, (nz, ny, nx), 2, 14)
    return jax.shard_map(
        run, mesh=mesh, in_specs=in_specs, out_specs=P(None, both, None), check_vma=False
    )
```

```python
import functools
import math

import jax
import jax.numpy as jnp
from jax import lax
from jax.experimental import pallas as pl
from jax.experimental.pallas import tpu as pltpu
from jax.sharding import PartitionSpec as P

MESH = pl.DeviceIdType.MESH
F32 = jnp.float32
BF16 = jnp.bfloat16
NT = (((1,), (1,)), ((), ()))


def dot_nt(a, b):
    return lax.dot_general(a, b, NT, preferred_element_type=F32)


def split3(v):
    hi = v.astype(BF16).astype(F32)
    rest = v - hi
    mid = rest.astype(BF16).astype(F32)
    return hi, mid, rest - mid


def kernel(
    dims,
    pos_hbm,
    den_hbm,
    off_hbm,
    cnt_hbm,
    ids_hbm,
    ops_hbm,
    lat_idx_hbm,
    up_hbm,
    m2l_hbm,
    lat_hbm,
    down_hbm,
    out_ref,
    pos_ref,
    den_ref,
    off_ref,
    cnt_ref,
    ids_ref,
    ops_ref,
    lat_idx_ref,
    up_v,
    m2l_v,
    lat_v,
    down_v,
    halo,
    id_s,
    op_s,
    csend,
    crecv,
    gz,
    stage,
    plane,
    psend,
    precv,
    b_s,
    a_s,
    l_s,
    at_s,
    m_s,
    acc_s,
    wsem,
    zsend,
    zrecv,
    xsend,
    xrecv,
    hsend,
    hrecv,
    osend,
    orecv,
):
    nz, ny, nx = dims
    planes = ny * nx
    per_z = 2 * ny
    leaf = lax.axis_index("leaf")
    rep = lax.axis_index("rep")
    z = leaf // per_z
    y = lax.rem(leaf // 2, ny)
    core = lax.rem(leaf, 2)
    box = leaf * nx + rep
    boxes = nz * ny * nx * 2
    me_p = y * nx + rep

    def z_peer(d):
        return (lax.rem(z + d, nz) * per_z + y * 2 + core, rep)

    def p_peer(d):
        return (
            z * per_z + lax.rem(y + d // nx, ny) * 2 + core,
            lax.rem(rep + lax.rem(d, nx), nx),
        )

    partner = (leaf + 1 - 2 * core, rep)
    after = lax.rem(box + 1, boxes)
    before = lax.rem(box + boxes - 1, boxes)
    after = (after // nx, lax.rem(after, nx))
    before = (before // nx, lax.rem(before, nx))

    loads = [
        pltpu.make_async_copy(src, dst, wsem.at[i])
        for i, (src, dst) in enumerate(
            [
                (pos_hbm, pos_ref),
                (den_hbm, den_ref),
                (up_hbm, up_v),
                (ids_hbm, ids_ref),
                (ops_hbm, ops_ref),
                (off_hbm, off_ref),
                (cnt_hbm, cnt_ref),
                (lat_idx_hbm, lat_idx_ref),
                (m2l_hbm, m2l_v),
                (lat_hbm, lat_v),
                (down_hbm, down_v),
            ]
        )
    ]
    for load in loads[:8]:
        load.start()

    leaves = pos_ref.shape[1]
    barrier = pltpu.get_barrier_semaphore()

    def greet(peer):
        pl.semaphore_signal(barrier, inc=1, device_id=peer, device_id_type=MESH)

    def far_first(k):
        return nz // 2 + ((k + 1) // 2) * (1 - 2 * lax.rem(k, 2))

    @pl.loop(0, nz - 1)
    def _(k):
        greet(z_peer(far_first(k)))

    @pl.loop(1, planes)
    def _(d):
        greet(p_peer(d))

    greet(partner)
    greet(after)
    greet(before)

    for load in loads[:2]:
        load.wait()
    x = [pos_ref[c] for c in range(3)]
    f = [den_ref[c] for c in range(3)]
    x2 = x[0] * x[0] + x[1] * x[1] + x[2] * x[2]
    damping = 1.0 / (1.0 + x2)
    summed = jnp.concatenate(
        [jnp.sum(f[c] * damping, axis=0, keepdims=True) for c in range(3)], axis=1
    )
    summed = jnp.broadcast_to(summed, (8, summed.shape[1])).astype(BF16)
    loads[2].wait()
    coarse = dot_nt(summed, up_v[...]).astype(BF16).astype(F32)
    gz[z] = coarse[0:1]

    pl.semaphore_wait(barrier, nz + planes + 1)

    def z_copy(d):
        return pltpu.make_async_remote_copy(
            src_ref=gz.at[z],
            dst_ref=gz.at[z],
            send_sem=zsend.at[d],
            recv_sem=zrecv.at[d],
            device_id=z_peer(d),
            device_id_type=MESH,
        )

    def p_copy(part, d):
        return pltpu.make_async_remote_copy(
            src_ref=plane.at[part, me_p],
            dst_ref=plane.at[part, me_p],
            send_sem=xsend.at[part, d],
            recv_sem=xrecv.at[part, d],
            device_id=p_peer(d),
            device_id_type=MESH,
        )

    @pl.loop(0, nz - 1)
    def _(k):
        z_copy(far_first(k)).start()

    def remote(src, dst, s, r, peer):
        return pltpu.make_async_remote_copy(
            src_ref=src, dst_ref=dst, send_sem=s, recv_sem=r, device_id=peer, device_id_type=MESH
        )

    high = pl.ds(leaves - 8, 8)
    halos = [
        remote(pos_ref.at[:, high, :], halo.at[0], hsend.at[0], hrecv.at[0], after),
        remote(den_ref.at[:, high, :], halo.at[1], hsend.at[1], hrecv.at[1], after),
        remote(pos_ref.at[:, 0:8, :], halo.at[2], hsend.at[2], hrecv.at[2], before),
        remote(den_ref.at[:, 0:8, :], halo.at[3], hsend.at[3], hrecv.at[3], before),
    ]
    for copy in halos:
        copy.start()
    for load in loads[8:]:
        load.start()

    for load in loads[3:7]:
        load.wait()
    half = boxes // 2
    group, quarter = nz // 2, nz // 4
    gb = group.bit_length() - 1
    id_s[...] = jnp.full(id_s.shape, -1, jnp.int32)
    op_s[...] = jnp.full(op_s.shape, -1, jnp.int32)
    nil = ids_ref.shape[1]
    id_s[0:1, 0:nil] = ids_ref[...]
    op_s[0:1, 0:nil] = ops_ref[...]
    ids = id_s[0:1, :]
    kinds = op_s[0:1, :]
    sx, sy = nx.bit_length() - 1, ny.bit_length() - 1
    id_x = ids & (nx - 1)
    id_core = (ids >> sx) & 1
    id_y = (ids >> (sx + 1)) & (ny - 1)
    id_z = ids >> (sx + 1 + sy)
    slot = (id_z - z + quarter) & (nz - 1)
    column = (slot >> gb) * (planes * group) + (id_y * nx + id_x) * group + (slot & (group - 1))
    column = jnp.where(ids < 0, -1, id_core * half + column)
    width = ids.shape[1]
    rows = lax.broadcasted_iota(jnp.int32, (boxes, width), 0)
    hot = jnp.where(rows == column, 1.0, 0.0).astype(BF16)
    kind_rows = lax.broadcasted_iota(jnp.int32, (8, width), 0)
    picks = jnp.where(kind_rows == kinds, 1.0, 0.0).astype(BF16)
    counts = dot_nt(picks, hot)
    one_row = lax.broadcasted_iota(jnp.int32, counts.shape, 0) == 4
    counts = jnp.where(one_row, 1.0, counts)
    left, right = counts[:, :half], counts[:, half:]
    first = core == 0
    csend[...] = jnp.where(first, right, left)
    own_counts = jnp.where(first, left, right)
    share = remote(csend, crecv, osend.at[0], orecv.at[0], partner)
    share.start()

    leaf_rows = lax.broadcasted_iota(jnp.int32, off_ref.shape, 0)
    slots = lax.broadcasted_iota(jnp.int32, off_ref.shape, 1)
    used = jnp.zeros(off_ref.shape, jnp.int32)
    for g in range(leaves):
        used = jnp.where(leaf_rows == g, cnt_ref[g], used)
    for o in range(5):
        hit = jnp.where((off_ref[...] == o - 2) & (slots < used), 1.0, 0.0)
        m_s[o] = jnp.broadcast_to(jnp.sum(hit, axis=1, keepdims=True), x2.shape)

    ones = jnp.ones(x2.shape, F32)
    zeros = jnp.zeros(x2.shape, F32)
    parts = [split3(v) for v in x]
    for s in range(3):
        for c in range(3):
            b_s[:, 3 * s + c, :] = parts[c][s]
    for s, v in enumerate(split3(x2 + 0.05)):
        b_s[:, 9 + s, :] = v
        b_s[:, 12 + s, :] = ones
    b_s[:, 15, :] = zeros

    def source_rows(lo, sx_, sf_):
        n = sx_[0].shape[0]
        at = pl.ds(lo, n)
        one, zero = jnp.ones(sx_[0].shape, F32), jnp.zeros(sx_[0].shape, F32)
        yy = [v.astype(BF16).astype(F32) for v in sx_]
        ff = [v.astype(BF16).astype(F32) for v in sf_]
        y2 = split3(yy[0] * yy[0] + yy[1] * yy[1] + yy[2] * yy[2])
        yf = split3(-(yy[0] * ff[0] + yy[1] * ff[1] + yy[2] * ff[2]))
        for s in range(3):
            for c in range(3):
                a_s[at, 3 * s + c, 0:128] = -2.0 * yy[c]
                a_s[at, 3 * s + c, 128:256] = ff[c]
            a_s[at, 9 + s, 0:128] = one
            a_s[at, 9 + s, 128:256] = zero
            a_s[at, 12 + s, 0:128] = y2[s]
            a_s[at, 12 + s, 128:256] = yf[s]
            l_s[at, s, 0:128] = ff[s]
            l_s[at, s, 128:256] = -yy[s]
        a_s[at, 15, 0:128] = zero
        a_s[at, 15, 128:256] = zero
        l_s[at, 3, 0:128] = zero
        l_s[at, 3, 128:256] = one
        for r in range(4, 8):
            l_s[at, r, 0:128] = zero
            l_s[at, r, 128:256] = zero

    def turn(lo, hi):
        @pl.loop(lo, hi)
        def _(i):
            at_s[i] = a_s[i].T.astype(BF16)

    source_rows(2, x, f)
    turn(2, leaves + 2)

    def near(lo, hi):
        @pl.loop(lo, hi)
        def _(g):
            target = b_s[g].astype(BF16)
            total = jnp.zeros((8, 128), F32)
            for o in range(5):
                qp = jnp.dot(at_s[g + o], target, preferred_element_type=F32)
                inv = lax.rsqrt(qp[0:128])
                w = qp[128:256] * (inv * inv * inv)
                pair = jnp.concatenate([inv, w], axis=0).astype(BF16)
                r = jnp.dot(l_s[g + o].astype(BF16), pair, preferred_element_type=F32)
                total = total + r * m_s[o, pl.ds(g, 1), :]
            acc_s[g] = total

    near(2, leaves - 2)

    def forward(part):
        for i in range(group):
            stage[i : i + 1, :] = gz[lax.rem(z + part * group + i - quarter + nz, nz)]
        plane[part, me_p] = stage[...].astype(BF16)

        @pl.loop(1, planes)
        def _(d):
            p_copy(part, d).start()

    def z_wait(lo, hi):
        @pl.loop(lo, hi)
        def _(d):
            z_copy(d).wait_recv()

    z_wait(1, quarter + 1)
    z_wait(nz - quarter + 1, nz)
    forward(0)

    for copy in halos:
        copy.wait_recv()
    source_rows(0, [halo[0, c, 6:8, :] for c in range(3)], [halo[1, c, 6:8, :] for c in range(3)])
    source_rows(
        leaves + 2, [halo[2, c, 0:2, :] for c in range(3)], [halo[3, c, 0:2, :] for c in range(3)]
    )
    turn(0, 2)
    turn(leaves + 2, leaves + 4)
    near(0, 2)
    near(leaves - 2, leaves)

    scale = 1.0 / (8.0 * math.pi)
    lever = acc_s[:, 3, :]
    near_part = [(acc_s[:, c, :] + x[c] * lever) * scale for c in range(3)]

    share.wait_recv()
    selector = jnp.concatenate([own_counts, crecv[...]], axis=0).astype(BF16)
    for load in loads[7:]:
        load.wait()

    z_wait(quarter + 1, nz - quarter + 1)
    forward(1)

    def gathered(part):
        @pl.loop(1, planes)
        def _(d):
            p_copy(part, d).wait_recv()

        n = planes * group
        blocks = plane[part].reshape(n, plane.shape[3])
        return jnp.dot(selector[:, part * n : (part + 1) * n], blocks, preferred_element_type=F32)

    partial = gathered(0)
    partial = partial + gathered(1)
    psend[...] = partial[8:16]
    swap = remote(psend, precv, osend.at[1], orecv.at[1], partner)
    swap.start()
    swap.wait_recv()
    grouped = (partial[0:8] + precv[...]).astype(BF16)

    def spread(t):
        return jnp.broadcast_to(grouped[t : t + 1].astype(F32), grouped.shape)

    lat_idx = lat_idx_ref[0]
    total = spread(4)
    local = jnp.zeros(grouped.shape, F32)
    for t in range(4):
        local = local + dot_nt(spread(t).astype(BF16), m2l_v[t])
    for i in range(2):
        kept = jnp.where(lat_idx == i, total, 0.0).astype(BF16)
        local = local + dot_nt(kept, lat_v[i])
    far = dot_nt(local.astype(BF16), down_v[...])
    for c in range(3):
        out_ref[c] = near_part[c] + damping * far[0:1, 128 * c : 128 * (c + 1)]

    @pl.loop(1, nz)
    def _(d):
        z_copy(d).wait_send()

    @pl.loop(1, planes)
    def _(d):
        p_copy(0, d).wait_send()
        p_copy(1, d).wait_send()

    for copy in halos + [share, swap]:
        copy.wait_send()


def body(dims, pos, den, off, cnt, ids, ops, lat_idx, up, m2l, lat, down):
    nz, ny, nx = dims
    planes = ny * nx
    boxes = nz * planes * 2
    leaves = pos.shape[1]
    coef = up.shape[0]
    vm = pl.BlockSpec(memory_space=pltpu.VMEM)
    hbm = pl.BlockSpec(memory_space=pltpu.HBM)
    dma = pltpu.SemaphoreType.DMA
    return pl.pallas_call(
        functools.partial(kernel, dims),
        out_shape=jax.ShapeDtypeStruct(pos.shape, F32),
        in_specs=[hbm] * 11,
        out_specs=vm,
        scratch_shapes=[
            pltpu.VMEM(pos.shape, F32),
            pltpu.VMEM(den.shape, F32),
            pltpu.VMEM(off.shape, jnp.int32),
            pltpu.SMEM(cnt.shape, jnp.int32),
            pltpu.VMEM(ids.shape, jnp.int32),
            pltpu.VMEM(ops.shape, jnp.int32),
            pltpu.SMEM(lat_idx.shape, jnp.int32),
            pltpu.VMEM(up.shape, BF16),
            pltpu.VMEM(m2l.shape, BF16),
            pltpu.VMEM(lat.shape, BF16),
            pltpu.VMEM(down.shape, BF16),
            pltpu.VMEM((4, 3, 8, 128), F32),
            pltpu.VMEM((8, 256), jnp.int32),
            pltpu.VMEM((8, 256), jnp.int32),
            pltpu.VMEM((8, boxes // 2), F32),
            pltpu.VMEM((8, boxes // 2), F32),
            pltpu.VMEM((nz, 1, coef), F32),
            pltpu.VMEM((nz // 2, coef), F32),
            pltpu.VMEM((2, planes, nz // 2, coef), BF16),
            pltpu.VMEM((8, coef), F32),
            pltpu.VMEM((8, coef), F32),
            pltpu.VMEM((leaves, 16, 128), F32),
            pltpu.VMEM((leaves + 4, 16, 256), F32),
            pltpu.VMEM((leaves + 4, 8, 256), F32),
            pltpu.VMEM((leaves + 4, 256, 16), BF16),
            pltpu.VMEM((5, leaves, 128), F32),
            pltpu.VMEM((leaves, 8, 128), F32),
            dma((11,)),
            dma((nz,)),
            dma((nz,)),
            dma((2, planes)),
            dma((2, planes)),
            dma((4,)),
            dma((4,)),
            dma((2,)),
            dma((2,)),
        ],
        compiler_params=pltpu.CompilerParams(
            collective_id=0, has_side_effects=True, vmem_limit_bytes=67043328
        ),
        name="fmm",
    )(pos, den, off, cnt, ids, ops, lat_idx, up, m2l, lat, down)


def solution(mesh):
    sizes = dict(mesh.shape)
    nx = sizes["rep"]
    ny = 4
    nz = sizes["leaf"] // (2 * ny)
    both = ("leaf", "rep")
    in_specs = (
        P(None, both, None),
        P(None, both, None),
        P(both, None),
        P(both),
        P(both, None),
        P(both, None),
        P(both),
        P(),
        P(),
        P(),
        P(),
    )
    run = functools.partial(body, (nz, ny, nx))
    return jax.shard_map(
        run, mesh=mesh, in_specs=in_specs, out_specs=P(None, both, None), check_vma=False
    )
```

```python
import functools
import math

import jax
import jax.numpy as jnp
from jax import lax
from jax.experimental import pallas as pl
from jax.experimental.pallas import tpu as pltpu
from jax.sharding import PartitionSpec as P

MESH = pl.DeviceIdType.MESH
F32 = jnp.float32
BF16 = jnp.bfloat16
NT = (((1,), (1,)), ((), ()))


def dot_nt(a, b):
    return lax.dot_general(a, b, NT, preferred_element_type=F32)


def split3(v):
    hi = v.astype(BF16).astype(F32)
    rest = v - hi
    mid = rest.astype(BF16).astype(F32)
    return hi, mid, rest - mid


def kernel(
    dims,
    ahead,
    pos_hbm,
    den_hbm,
    off_hbm,
    cnt_hbm,
    ids_hbm,
    ops_hbm,
    lat_idx_hbm,
    up_hbm,
    m2l_hbm,
    lat_hbm,
    down_hbm,
    out_ref,
    pos_ref,
    den_ref,
    off_ref,
    cnt_ref,
    ids_ref,
    ops_ref,
    lat_idx_ref,
    up_v,
    m2l_v,
    lat_v,
    down_v,
    halo,
    id_s,
    op_s,
    csend,
    crecv,
    gz,
    stage,
    plane,
    psend,
    precv,
    b_s,
    a_s,
    l_s,
    at_s,
    m_s,
    acc_s,
    wsem,
    zsend,
    zrecv,
    xsend,
    xrecv,
    hsend,
    hrecv,
    osend,
    orecv,
):
    nz, ny, nx = dims
    planes = ny * nx
    per_z = 2 * ny
    leaf = lax.axis_index("leaf")
    rep = lax.axis_index("rep")
    z = leaf // per_z
    y = lax.rem(leaf // 2, ny)
    core = lax.rem(leaf, 2)
    box = leaf * nx + rep
    boxes = nz * ny * nx * 2
    me_p = y * nx + rep

    def z_peer(d):
        return (lax.rem(z + d, nz) * per_z + y * 2 + core, rep)

    def p_peer(d):
        return (
            z * per_z + lax.rem(y + d // nx, ny) * 2 + core,
            lax.rem(rep + lax.rem(d, nx), nx),
        )

    partner = (leaf + 1 - 2 * core, rep)
    after = lax.rem(box + 1, boxes)
    before = lax.rem(box + boxes - 1, boxes)
    after = (after // nx, lax.rem(after, nx))
    before = (before // nx, lax.rem(before, nx))

    loads = [
        pltpu.make_async_copy(src, dst, wsem.at[i])
        for i, (src, dst) in enumerate(
            [
                (pos_hbm, pos_ref),
                (den_hbm, den_ref),
                (up_hbm, up_v),
                (ids_hbm, ids_ref),
                (ops_hbm, ops_ref),
                (off_hbm, off_ref),
                (cnt_hbm, cnt_ref),
                (lat_idx_hbm, lat_idx_ref),
                (m2l_hbm, m2l_v),
                (lat_hbm, lat_v),
                (down_hbm, down_v),
            ]
        )
    ]
    for load in loads[:8]:
        load.start()

    leaves = pos_ref.shape[1]
    barrier = pltpu.get_barrier_semaphore()

    def greet(peer):
        pl.semaphore_signal(barrier, inc=1, device_id=peer, device_id_type=MESH)

    def far_first(k):
        return nz // 2 + ((k + 1) // 2) * (1 - 2 * lax.rem(k, 2))

    @pl.loop(0, nz - 1)
    def _(k):
        greet(z_peer(far_first(k)))

    @pl.loop(1, planes)
    def _(d):
        greet(p_peer(d))

    greet(partner)
    greet(after)
    greet(before)

    for load in loads[:2]:
        load.wait()
    x = [pos_ref[c] for c in range(3)]
    f = [den_ref[c] for c in range(3)]
    x2 = x[0] * x[0] + x[1] * x[1] + x[2] * x[2]
    damping = 1.0 / (1.0 + x2)
    summed = jnp.concatenate(
        [jnp.sum(f[c] * damping, axis=0, keepdims=True) for c in range(3)], axis=1
    )
    summed = jnp.broadcast_to(summed, (8, summed.shape[1])).astype(BF16)
    loads[2].wait()
    coarse = dot_nt(summed, up_v[...]).astype(BF16).astype(F32)
    gz[z] = coarse[0:1]

    def source_rows(lo, sx_, sf_):
        n = sx_[0].shape[0]
        at = pl.ds(lo, n)
        one, zero = jnp.ones(sx_[0].shape, F32), jnp.zeros(sx_[0].shape, F32)
        yy = [v.astype(BF16).astype(F32) for v in sx_]
        ff = [v.astype(BF16).astype(F32) for v in sf_]
        y2 = split3(yy[0] * yy[0] + yy[1] * yy[1] + yy[2] * yy[2])
        yf = split3(-(yy[0] * ff[0] + yy[1] * ff[1] + yy[2] * ff[2]))
        for s in range(3):
            for c in range(3):
                a_s[at, 3 * s + c, 0:128] = -2.0 * yy[c]
                a_s[at, 3 * s + c, 128:256] = ff[c]
            a_s[at, 9 + s, 0:128] = one
            a_s[at, 9 + s, 128:256] = zero
            a_s[at, 12 + s, 0:128] = y2[s]
            a_s[at, 12 + s, 128:256] = yf[s]
            l_s[at, s, 0:128] = ff[s]
            l_s[at, s, 128:256] = -yy[s]
        a_s[at, 15, 0:128] = zero
        a_s[at, 15, 128:256] = zero
        l_s[at, 3, 0:128] = zero
        l_s[at, 3, 128:256] = one
        for r in range(4, 8):
            l_s[at, r, 0:128] = zero
            l_s[at, r, 128:256] = zero

    def turn(lo, hi):
        @pl.loop(lo, hi)
        def _(i):
            at_s[i] = a_s[i].T.astype(BF16)

    def near(lo, hi):
        @pl.loop(lo, hi)
        def _(j):
            g = 2 * j
            pair = [b_s[g].astype(BF16), b_s[g + 1].astype(BF16)]
            both = jnp.concatenate(pair, axis=1)
            totals = [jnp.zeros((8, 128), F32)] * 2
            for o in range(6):
                used_by = [t for t in range(2) if 0 <= o - t < 5]
                target = both if len(used_by) == 2 else pair[used_by[0]]
                qp = jnp.dot(at_s[g + o], target, preferred_element_type=F32)
                inv = lax.rsqrt(qp[0:128])
                w = qp[128:256] * (inv * inv * inv)
                terms = jnp.concatenate([inv, w], axis=0).astype(BF16)
                r = jnp.dot(l_s[g + o].astype(BF16), terms, preferred_element_type=F32)
                for i, t in enumerate(used_by):
                    weight = m_s[o - t, pl.ds(g + t, 1), :]
                    totals[t] = totals[t] + r[:, 128 * i : 128 * (i + 1)] * weight
            acc_s[g] = totals[0]
            acc_s[g + 1] = totals[1]

    def inner():
        for load in loads[5:7]:
            load.wait()
        leaf_rows = lax.broadcasted_iota(jnp.int32, off_ref.shape, 0)
        slots = lax.broadcasted_iota(jnp.int32, off_ref.shape, 1)
        used = jnp.zeros(off_ref.shape, jnp.int32)
        for g in range(leaves):
            used = jnp.where(leaf_rows == g, cnt_ref[g], used)
        for o in range(5):
            hit = jnp.where((off_ref[...] == o - 2) & (slots < used), 1.0, 0.0)
            m_s[o] = jnp.broadcast_to(jnp.sum(hit, axis=1, keepdims=True), x2.shape)

        ones = jnp.ones(x2.shape, F32)
        zeros = jnp.zeros(x2.shape, F32)
        parts = [split3(v) for v in x]
        for s in range(3):
            for c in range(3):
                b_s[:, 3 * s + c, :] = parts[c][s]
        for s, v in enumerate(split3(x2 + 0.05)):
            b_s[:, 9 + s, :] = v
            b_s[:, 12 + s, :] = ones
        b_s[:, 15, :] = zeros
        source_rows(2, x, f)
        turn(2, leaves + 2)
        near(1, leaves // 2 - 1)

    @pl.when(z < ahead)
    def _():
        inner()

    pl.semaphore_wait(barrier, nz + planes + 1)

    def z_copy(d):
        return pltpu.make_async_remote_copy(
            src_ref=gz.at[z],
            dst_ref=gz.at[z],
            send_sem=zsend.at[d],
            recv_sem=zrecv.at[d],
            device_id=z_peer(d),
            device_id_type=MESH,
        )

    def p_copy(part, d):
        return pltpu.make_async_remote_copy(
            src_ref=plane.at[part, me_p],
            dst_ref=plane.at[part, me_p],
            send_sem=xsend.at[part, d],
            recv_sem=xrecv.at[part, d],
            device_id=p_peer(d),
            device_id_type=MESH,
        )

    @pl.loop(0, nz - 1)
    def _(k):
        z_copy(far_first(k)).start()

    def remote(src, dst, s, r, peer):
        return pltpu.make_async_remote_copy(
            src_ref=src, dst_ref=dst, send_sem=s, recv_sem=r, device_id=peer, device_id_type=MESH
        )

    high = pl.ds(leaves - 8, 8)
    halos = [
        remote(pos_ref.at[:, high, :], halo.at[0], hsend.at[0], hrecv.at[0], after),
        remote(den_ref.at[:, high, :], halo.at[1], hsend.at[1], hrecv.at[1], after),
        remote(pos_ref.at[:, 0:8, :], halo.at[2], hsend.at[2], hrecv.at[2], before),
        remote(den_ref.at[:, 0:8, :], halo.at[3], hsend.at[3], hrecv.at[3], before),
    ]
    for copy in halos:
        copy.start()
    for load in loads[8:]:
        load.start()

    for load in loads[3:5]:
        load.wait()
    half = boxes // 2
    group, quarter = nz // 2, nz // 4
    gb = group.bit_length() - 1
    id_s[...] = jnp.full(id_s.shape, -1, jnp.int32)
    op_s[...] = jnp.full(op_s.shape, -1, jnp.int32)
    nil = ids_ref.shape[1]
    id_s[0:1, 0:nil] = ids_ref[...]
    op_s[0:1, 0:nil] = ops_ref[...]
    ids = id_s[0:1, :]
    kinds = op_s[0:1, :]
    sx, sy = nx.bit_length() - 1, ny.bit_length() - 1
    id_x = ids & (nx - 1)
    id_core = (ids >> sx) & 1
    id_y = (ids >> (sx + 1)) & (ny - 1)
    id_z = ids >> (sx + 1 + sy)
    slot = (id_z - z + quarter) & (nz - 1)
    column = (slot >> gb) * (planes * group) + (id_y * nx + id_x) * group + (slot & (group - 1))
    column = jnp.where(ids < 0, -1, id_core * half + column)
    width = ids.shape[1]
    rows = lax.broadcasted_iota(jnp.int32, (boxes, width), 0)
    hot = jnp.where(rows == column, 1.0, 0.0).astype(BF16)
    kind_rows = lax.broadcasted_iota(jnp.int32, (8, width), 0)
    picks = jnp.where(kind_rows == kinds, 1.0, 0.0).astype(BF16)
    counts = dot_nt(picks, hot)
    one_row = lax.broadcasted_iota(jnp.int32, counts.shape, 0) == 4
    counts = jnp.where(one_row, 1.0, counts)
    left, right = counts[:, :half], counts[:, half:]
    first = core == 0
    csend[...] = jnp.where(first, right, left)
    own_counts = jnp.where(first, left, right)
    share = remote(csend, crecv, osend.at[0], orecv.at[0], partner)
    share.start()

    @pl.when(z >= ahead)
    def _():
        inner()


    def forward(part):
        for i in range(group):
            stage[i : i + 1, :] = gz[lax.rem(z + part * group + i - quarter + nz, nz)]
        plane[part, me_p] = stage[...].astype(BF16)

        @pl.loop(1, planes)
        def _(d):
            p_copy(part, d).start()

    def z_wait(lo, hi):
        @pl.loop(lo, hi)
        def _(d):
            z_copy(d).wait_recv()

    z_wait(1, quarter + 1)
    z_wait(nz - quarter + 1, nz)
    forward(0)

    for copy in halos:
        copy.wait_recv()
    source_rows(0, [halo[0, c, 6:8, :] for c in range(3)], [halo[1, c, 6:8, :] for c in range(3)])
    source_rows(
        leaves + 2, [halo[2, c, 0:2, :] for c in range(3)], [halo[3, c, 0:2, :] for c in range(3)]
    )
    turn(0, 2)
    turn(leaves + 2, leaves + 4)
    near(0, 1)
    near(leaves // 2 - 1, leaves // 2)

    scale = 1.0 / (8.0 * math.pi)
    lever = acc_s[:, 3, :]
    near_part = [(acc_s[:, c, :] + x[c] * lever) * scale for c in range(3)]

    share.wait_recv()
    selector = jnp.concatenate([own_counts, crecv[...]], axis=0).astype(BF16)
    for load in loads[7:]:
        load.wait()

    z_wait(quarter + 1, nz - quarter + 1)
    forward(1)

    def gathered(part):
        @pl.loop(1, planes)
        def _(d):
            p_copy(part, d).wait_recv()

        n = planes * group
        blocks = plane[part].reshape(n, plane.shape[3])
        return jnp.dot(selector[:, part * n : (part + 1) * n], blocks, preferred_element_type=F32)

    partial = gathered(0)
    partial = partial + gathered(1)
    psend[...] = partial[8:16]
    swap = remote(psend, precv, osend.at[1], orecv.at[1], partner)
    swap.start()
    swap.wait_recv()
    grouped = (partial[0:8] + precv[...]).astype(BF16)

    def spread(t):
        return jnp.broadcast_to(grouped[t : t + 1].astype(F32), grouped.shape)

    lat_idx = lat_idx_ref[0]
    total = spread(4)
    local = jnp.zeros(grouped.shape, F32)
    for t in range(4):
        local = local + dot_nt(spread(t).astype(BF16), m2l_v[t])
    for i in range(2):
        kept = jnp.where(lat_idx == i, total, 0.0).astype(BF16)
        local = local + dot_nt(kept, lat_v[i])
    far = dot_nt(local.astype(BF16), down_v[...])
    for c in range(3):
        out_ref[c] = near_part[c] + damping * far[0:1, 128 * c : 128 * (c + 1)]

    @pl.loop(1, nz)
    def _(d):
        z_copy(d).wait_send()

    @pl.loop(1, planes)
    def _(d):
        p_copy(0, d).wait_send()
        p_copy(1, d).wait_send()

    for copy in halos + [share, swap]:
        copy.wait_send()


def body(dims, ahead, pos, den, off, cnt, ids, ops, lat_idx, up, m2l, lat, down):
    nz, ny, nx = dims
    planes = ny * nx
    boxes = nz * planes * 2
    leaves = pos.shape[1]
    coef = up.shape[0]
    vm = pl.BlockSpec(memory_space=pltpu.VMEM)
    hbm = pl.BlockSpec(memory_space=pltpu.HBM)
    dma = pltpu.SemaphoreType.DMA
    return pl.pallas_call(
        functools.partial(kernel, dims, ahead),
        out_shape=jax.ShapeDtypeStruct(pos.shape, F32),
        in_specs=[hbm] * 11,
        out_specs=vm,
        scratch_shapes=[
            pltpu.VMEM(pos.shape, F32),
            pltpu.VMEM(den.shape, F32),
            pltpu.VMEM(off.shape, jnp.int32),
            pltpu.SMEM(cnt.shape, jnp.int32),
            pltpu.VMEM(ids.shape, jnp.int32),
            pltpu.VMEM(ops.shape, jnp.int32),
            pltpu.SMEM(lat_idx.shape, jnp.int32),
            pltpu.VMEM(up.shape, BF16),
            pltpu.VMEM(m2l.shape, BF16),
            pltpu.VMEM(lat.shape, BF16),
            pltpu.VMEM(down.shape, BF16),
            pltpu.VMEM((4, 3, 8, 128), F32),
            pltpu.VMEM((8, 256), jnp.int32),
            pltpu.VMEM((8, 256), jnp.int32),
            pltpu.VMEM((8, boxes // 2), F32),
            pltpu.VMEM((8, boxes // 2), F32),
            pltpu.VMEM((nz, 1, coef), F32),
            pltpu.VMEM((nz // 2, coef), F32),
            pltpu.VMEM((2, planes, nz // 2, coef), BF16),
            pltpu.VMEM((8, coef), F32),
            pltpu.VMEM((8, coef), F32),
            pltpu.VMEM((leaves, 16, 128), F32),
            pltpu.VMEM((leaves + 4, 16, 256), F32),
            pltpu.VMEM((leaves + 4, 8, 256), F32),
            pltpu.VMEM((leaves + 4, 256, 16), BF16),
            pltpu.VMEM((5, leaves, 128), F32),
            pltpu.VMEM((leaves, 8, 128), F32),
            dma((11,)),
            dma((nz,)),
            dma((nz,)),
            dma((2, planes)),
            dma((2, planes)),
            dma((4,)),
            dma((4,)),
            dma((2,)),
            dma((2,)),
        ],
        compiler_params=pltpu.CompilerParams(
            collective_id=0, has_side_effects=True, vmem_limit_bytes=67043328
        ),
        name="fmm",
    )(pos, den, off, cnt, ids, ops, lat_idx, up, m2l, lat, down)


def solution(mesh):
    sizes = dict(mesh.shape)
    nx = sizes["rep"]
    ny = 4
    nz = sizes["leaf"] // (2 * ny)
    both = ("leaf", "rep")
    in_specs = (
        P(None, both, None),
        P(None, both, None),
        P(both, None),
        P(both),
        P(both, None),
        P(both, None),
        P(both),
        P(),
        P(),
        P(),
        P(),
    )
    run = functools.partial(body, (nz, ny, nx), nz // 4 + 1)
    return jax.shard_map(
        run, mesh=mesh, in_specs=in_specs, out_specs=P(None, both, None), check_vma=False
    )
```

```python
import functools
import math

import jax
import jax.numpy as jnp
from jax import lax
from jax.experimental import pallas as pl
from jax.experimental.pallas import tpu as pltpu
from jax.sharding import PartitionSpec as P

MESH = pl.DeviceIdType.MESH
F32 = jnp.float32
BF16 = jnp.bfloat16
NT = (((1,), (1,)), ((), ()))


def dot_nt(a, b):
    return lax.dot_general(a, b, NT, preferred_element_type=F32)


def split3(v):
    hi = v.astype(BF16).astype(F32)
    rest = v - hi
    mid = rest.astype(BF16).astype(F32)
    return hi, mid, rest - mid


def kernel(
    dims,
    ahead,
    pos_hbm,
    den_hbm,
    off_hbm,
    cnt_hbm,
    ids_hbm,
    ops_hbm,
    lat_idx_hbm,
    up_hbm,
    m2l_hbm,
    lat_hbm,
    down_hbm,
    out_ref,
    pos_ref,
    den_ref,
    off_ref,
    cnt_ref,
    ids_ref,
    ops_ref,
    lat_idx_ref,
    up_v,
    m2l_v,
    lat_v,
    down_v,
    halo,
    id_s,
    op_s,
    csend,
    crecv,
    gz,
    stage,
    plane,
    psend,
    precv,
    b_s,
    a_s,
    l_s,
    at_s,
    m_s,
    acc_s,
    wsem,
    zsend,
    zrecv,
    xsend,
    xrecv,
    hsend,
    hrecv,
    osend,
    orecv,
):
    nz, ny, nx = dims
    planes = ny * nx
    per_z = 2 * ny
    leaf = lax.axis_index("leaf")
    rep = lax.axis_index("rep")
    z = leaf // per_z
    y = lax.rem(leaf // 2, ny)
    core = lax.rem(leaf, 2)
    box = leaf * nx + rep
    boxes = nz * ny * nx * 2
    me_p = y * nx + rep

    def z_peer(d):
        return (lax.rem(z + d, nz) * per_z + y * 2 + core, rep)

    def p_peer(d):
        return (
            z * per_z + lax.rem(y + d // nx, ny) * 2 + core,
            lax.rem(rep + lax.rem(d, nx), nx),
        )

    partner = (leaf + 1 - 2 * core, rep)
    after = lax.rem(box + 1, boxes)
    before = lax.rem(box + boxes - 1, boxes)
    after = (after // nx, lax.rem(after, nx))
    before = (before // nx, lax.rem(before, nx))

    loads = [
        pltpu.make_async_copy(src, dst, wsem.at[i])
        for i, (src, dst) in enumerate(
            [
                (pos_hbm, pos_ref),
                (den_hbm, den_ref),
                (up_hbm, up_v),
                (ids_hbm, ids_ref),
                (ops_hbm, ops_ref),
                (off_hbm, off_ref),
                (cnt_hbm, cnt_ref),
                (lat_idx_hbm, lat_idx_ref),
                (m2l_hbm, m2l_v),
                (lat_hbm, lat_v),
                (down_hbm, down_v),
            ]
        )
    ]
    for load in loads[:8]:
        load.start()

    leaves = pos_ref.shape[1]
    barrier = pltpu.get_barrier_semaphore()

    def greet(peer):
        pl.semaphore_signal(barrier, inc=1, device_id=peer, device_id_type=MESH)

    def far_first(k):
        return nz // 2 + ((k + 1) // 2) * (1 - 2 * lax.rem(k, 2))

    @pl.loop(0, nz - 1)
    def _(k):
        greet(z_peer(far_first(k)))

    @pl.loop(1, planes)
    def _(d):
        greet(p_peer(d))

    greet(partner)
    greet(after)
    greet(before)

    for load in loads[:2]:
        load.wait()
    x = [pos_ref[c] for c in range(3)]
    f = [den_ref[c] for c in range(3)]
    x2 = x[0] * x[0] + x[1] * x[1] + x[2] * x[2]
    damping = 1.0 / (1.0 + x2)
    summed = jnp.concatenate(
        [jnp.sum(f[c] * damping, axis=0, keepdims=True) for c in range(3)], axis=1
    )
    summed = jnp.broadcast_to(summed, (8, summed.shape[1])).astype(BF16)
    loads[2].wait()
    coarse = dot_nt(summed, up_v[...]).astype(BF16).astype(F32)
    gz[z] = coarse[0:1]

    def source_rows(lo, sx_, sf_):
        n = sx_[0].shape[0]
        at = pl.ds(lo, n)
        one, zero = jnp.ones(sx_[0].shape, F32), jnp.zeros(sx_[0].shape, F32)
        yy = [v.astype(BF16).astype(F32) for v in sx_]
        ff = [v.astype(BF16).astype(F32) for v in sf_]
        y2 = split3(yy[0] * yy[0] + yy[1] * yy[1] + yy[2] * yy[2])
        yf = split3(-(yy[0] * ff[0] + yy[1] * ff[1] + yy[2] * ff[2]))
        for s in range(3):
            for c in range(3):
                a_s[at, 3 * s + c, 0:128] = -2.0 * yy[c]
                a_s[at, 3 * s + c, 128:256] = ff[c]
            a_s[at, 9 + s, 0:128] = one
            a_s[at, 9 + s, 128:256] = zero
            a_s[at, 12 + s, 0:128] = y2[s]
            a_s[at, 12 + s, 128:256] = yf[s]
            l_s[at, s, 0:128] = ff[s]
            l_s[at, s, 128:256] = -yy[s]
        a_s[at, 15, 0:128] = zero
        a_s[at, 15, 128:256] = zero
        l_s[at, 3, 0:128] = zero
        l_s[at, 3, 128:256] = one
        for r in range(4, 8):
            l_s[at, r, 0:128] = zero
            l_s[at, r, 128:256] = zero

    def turn(lo, hi):
        @pl.loop(lo, hi)
        def _(i):
            at_s[i] = a_s[i].T.astype(BF16)

    def near(lo, hi):
        @pl.loop(lo, hi)
        def _(j):
            g = 2 * j
            pair = [b_s[g].astype(BF16), b_s[g + 1].astype(BF16)]
            both = jnp.concatenate(pair, axis=1)
            totals = [jnp.zeros((8, 128), F32)] * 2
            for o in range(6):
                used_by = [t for t in range(2) if 0 <= o - t < 5]
                target = both if len(used_by) == 2 else pair[used_by[0]]
                qp = jnp.dot(at_s[g + o], target, preferred_element_type=F32)
                inv = lax.rsqrt(qp[0:128])
                w = qp[128:256] * (inv * inv * inv)
                terms = jnp.concatenate([inv, w], axis=0).astype(BF16)
                r = jnp.dot(l_s[g + o].astype(BF16), terms, preferred_element_type=F32)
                for i, t in enumerate(used_by):
                    weight = m_s[o - t, pl.ds(g + t, 1), :]
                    totals[t] = totals[t] + r[:, 128 * i : 128 * (i + 1)] * weight
            acc_s[g] = totals[0]
            acc_s[g + 1] = totals[1]

    def inner():
        for load in loads[5:7]:
            load.wait()
        leaf_rows = lax.broadcasted_iota(jnp.int32, off_ref.shape, 0)
        slots = lax.broadcasted_iota(jnp.int32, off_ref.shape, 1)
        used = jnp.zeros(off_ref.shape, jnp.int32)
        for g in range(leaves):
            used = jnp.where(leaf_rows == g, cnt_ref[g], used)
        for o in range(5):
            hit = jnp.where((off_ref[...] == o - 2) & (slots < used), 1.0, 0.0)
            m_s[o] = jnp.broadcast_to(jnp.sum(hit, axis=1, keepdims=True), x2.shape)

        ones = jnp.ones(x2.shape, F32)
        zeros = jnp.zeros(x2.shape, F32)
        parts = [split3(v) for v in x]
        for s in range(3):
            for c in range(3):
                b_s[:, 3 * s + c, :] = parts[c][s]
        for s, v in enumerate(split3(x2 + 0.05)):
            b_s[:, 9 + s, :] = v
            b_s[:, 12 + s, :] = ones
        b_s[:, 15, :] = zeros
        source_rows(2, x, f)
        turn(2, leaves + 2)
        near(1, leaves // 2 - 1)

    @pl.when(z < ahead)
    def _():
        inner()

    pl.semaphore_wait(barrier, nz + planes + 1)

    def z_copy(d):
        return pltpu.make_async_remote_copy(
            src_ref=gz.at[z],
            dst_ref=gz.at[z],
            send_sem=zsend.at[d],
            recv_sem=zrecv.at[d],
            device_id=z_peer(d),
            device_id_type=MESH,
        )

    def p_copy(part, d):
        return pltpu.make_async_remote_copy(
            src_ref=plane.at[part, me_p],
            dst_ref=plane.at[part, me_p],
            send_sem=xsend.at[part, d],
            recv_sem=xrecv.at[part, d],
            device_id=p_peer(d),
            device_id_type=MESH,
        )

    @pl.loop(0, nz - 1)
    def _(k):
        z_copy(far_first(k)).start()

    def remote(src, dst, s, r, peer):
        return pltpu.make_async_remote_copy(
            src_ref=src, dst_ref=dst, send_sem=s, recv_sem=r, device_id=peer, device_id_type=MESH
        )

    high = pl.ds(leaves - 8, 8)
    halos = [
        remote(pos_ref.at[:, high, :], halo.at[0], hsend.at[0], hrecv.at[0], after),
        remote(den_ref.at[:, high, :], halo.at[1], hsend.at[1], hrecv.at[1], after),
        remote(pos_ref.at[:, 0:8, :], halo.at[2], hsend.at[2], hrecv.at[2], before),
        remote(den_ref.at[:, 0:8, :], halo.at[3], hsend.at[3], hrecv.at[3], before),
    ]
    for copy in halos:
        copy.start()
    for load in loads[8:]:
        load.start()

    for load in loads[3:5]:
        load.wait()
    half = boxes // 2
    group, quarter = nz // 2, nz // 4
    gb = group.bit_length() - 1
    id_s[...] = jnp.full(id_s.shape, -1, jnp.int32)
    op_s[...] = jnp.full(op_s.shape, -1, jnp.int32)
    nil = ids_ref.shape[1]
    id_s[0:1, 0:nil] = ids_ref[...]
    op_s[0:1, 0:nil] = ops_ref[...]
    ids = id_s[0:1, :]
    kinds = op_s[0:1, :]
    sx, sy = nx.bit_length() - 1, ny.bit_length() - 1
    id_x = ids & (nx - 1)
    id_core = (ids >> sx) & 1
    id_y = (ids >> (sx + 1)) & (ny - 1)
    id_z = ids >> (sx + 1 + sy)
    slot = (id_z - z + quarter) & (nz - 1)
    column = (slot >> gb) * (planes * group) + (id_y * nx + id_x) * group + (slot & (group - 1))
    column = jnp.where(ids < 0, -1, id_core * half + column)
    width = ids.shape[1]
    rows = lax.broadcasted_iota(jnp.int32, (boxes, width), 0)
    hot = jnp.where(rows == column, 1.0, 0.0).astype(BF16)
    kind_rows = lax.broadcasted_iota(jnp.int32, (8, width), 0)
    picks = jnp.where(kind_rows == kinds, 1.0, 0.0).astype(BF16)
    counts = dot_nt(picks, hot)
    one_row = lax.broadcasted_iota(jnp.int32, counts.shape, 0) == 4
    counts = jnp.where(one_row, 1.0, counts)
    left, right = counts[:, :half], counts[:, half:]
    first = core == 0
    csend[...] = jnp.where(first, right, left)
    own_counts = jnp.where(first, left, right)
    share = remote(csend, crecv, osend.at[0], orecv.at[0], partner)
    share.start()

    @pl.when(z >= ahead)
    def _():
        inner()


    def forward(part):
        for i in range(group):
            stage[i : i + 1, :] = gz[lax.rem(z + part * group + i - quarter + nz, nz)]
        plane[part, me_p] = stage[...].astype(BF16)

        @pl.loop(1, planes)
        def _(d):
            p_copy(part, d).start()

    def z_wait(lo, hi):
        @pl.loop(lo, hi)
        def _(d):
            z_copy(d).wait_recv()

    z_wait(1, quarter + 1)
    z_wait(nz - quarter + 1, nz)
    forward(0)


    share.wait_recv()
    selector = jnp.concatenate([own_counts, crecv[...]], axis=0).astype(BF16)
    for load in loads[7:]:
        load.wait()

    z_wait(quarter + 1, nz - quarter + 1)
    forward(1)
    for copy in halos:
        copy.wait_recv()
    source_rows(0, [halo[0, c, 6:8, :] for c in range(3)], [halo[1, c, 6:8, :] for c in range(3)])
    source_rows(
        leaves + 2, [halo[2, c, 0:2, :] for c in range(3)], [halo[3, c, 0:2, :] for c in range(3)]
    )
    turn(0, 2)
    turn(leaves + 2, leaves + 4)
    near(0, 1)
    near(leaves // 2 - 1, leaves // 2)

    scale = 1.0 / (8.0 * math.pi)
    lever = acc_s[:, 3, :]
    near_part = [(acc_s[:, c, :] + x[c] * lever) * scale for c in range(3)]

    def gathered(part):
        @pl.loop(1, planes)
        def _(d):
            p_copy(part, d).wait_recv()

        n = planes * group
        blocks = plane[part].reshape(n, plane.shape[3])
        return jnp.dot(selector[:, part * n : (part + 1) * n], blocks, preferred_element_type=F32)

    partial = gathered(0)
    partial = partial + gathered(1)
    psend[...] = partial[8:16]
    swap = remote(psend, precv, osend.at[1], orecv.at[1], partner)
    swap.start()
    swap.wait_recv()
    grouped = (partial[0:8] + precv[...]).astype(BF16)

    def spread(t):
        return jnp.broadcast_to(grouped[t : t + 1].astype(F32), grouped.shape)

    lat_idx = lat_idx_ref[0]
    total = spread(4)
    local = jnp.zeros(grouped.shape, F32)
    for t in range(4):
        local = local + dot_nt(spread(t).astype(BF16), m2l_v[t])
    for i in range(2):
        kept = jnp.where(lat_idx == i, total, 0.0).astype(BF16)
        local = local + dot_nt(kept, lat_v[i])
    far = dot_nt(local.astype(BF16), down_v[...])
    for c in range(3):
        out_ref[c] = near_part[c] + damping * far[0:1, 128 * c : 128 * (c + 1)]

    @pl.loop(1, nz)
    def _(d):
        z_copy(d).wait_send()

    @pl.loop(1, planes)
    def _(d):
        p_copy(0, d).wait_send()
        p_copy(1, d).wait_send()

    for copy in halos + [share, swap]:
        copy.wait_send()


def body(dims, ahead, pos, den, off, cnt, ids, ops, lat_idx, up, m2l, lat, down):
    nz, ny, nx = dims
    planes = ny * nx
    boxes = nz * planes * 2
    leaves = pos.shape[1]
    coef = up.shape[0]
    vm = pl.BlockSpec(memory_space=pltpu.VMEM)
    hbm = pl.BlockSpec(memory_space=pltpu.HBM)
    dma = pltpu.SemaphoreType.DMA
    return pl.pallas_call(
        functools.partial(kernel, dims, ahead),
        out_shape=jax.ShapeDtypeStruct(pos.shape, F32),
        in_specs=[hbm] * 11,
        out_specs=vm,
        scratch_shapes=[
            pltpu.VMEM(pos.shape, F32),
            pltpu.VMEM(den.shape, F32),
            pltpu.VMEM(off.shape, jnp.int32),
            pltpu.SMEM(cnt.shape, jnp.int32),
            pltpu.VMEM(ids.shape, jnp.int32),
            pltpu.VMEM(ops.shape, jnp.int32),
            pltpu.SMEM(lat_idx.shape, jnp.int32),
            pltpu.VMEM(up.shape, BF16),
            pltpu.VMEM(m2l.shape, BF16),
            pltpu.VMEM(lat.shape, BF16),
            pltpu.VMEM(down.shape, BF16),
            pltpu.VMEM((4, 3, 8, 128), F32),
            pltpu.VMEM((8, 256), jnp.int32),
            pltpu.VMEM((8, 256), jnp.int32),
            pltpu.VMEM((8, boxes // 2), F32),
            pltpu.VMEM((8, boxes // 2), F32),
            pltpu.VMEM((nz, 1, coef), F32),
            pltpu.VMEM((nz // 2, coef), F32),
            pltpu.VMEM((2, planes, nz // 2, coef), BF16),
            pltpu.VMEM((8, coef), F32),
            pltpu.VMEM((8, coef), F32),
            pltpu.VMEM((leaves, 16, 128), F32),
            pltpu.VMEM((leaves + 4, 16, 256), F32),
            pltpu.VMEM((leaves + 4, 8, 256), F32),
            pltpu.VMEM((leaves + 4, 256, 16), BF16),
            pltpu.VMEM((5, leaves, 128), F32),
            pltpu.VMEM((leaves, 8, 128), F32),
            dma((11,)),
            dma((nz,)),
            dma((nz,)),
            dma((2, planes)),
            dma((2, planes)),
            dma((4,)),
            dma((4,)),
            dma((2,)),
            dma((2,)),
        ],
        compiler_params=pltpu.CompilerParams(
            collective_id=0, has_side_effects=True, vmem_limit_bytes=67043328
        ),
        name="fmm",
    )(pos, den, off, cnt, ids, ops, lat_idx, up, m2l, lat, down)


def solution(mesh):
    sizes = dict(mesh.shape)
    nx = sizes["rep"]
    ny = 4
    nz = sizes["leaf"] // (2 * ny)
    both = ("leaf", "rep")
    in_specs = (
        P(None, both, None),
        P(None, both, None),
        P(both, None),
        P(both),
        P(both, None),
        P(both, None),
        P(both),
        P(),
        P(),
        P(),
        P(),
    )
    run = functools.partial(body, (nz, ny, nx), nz // 4 + 1)
    return jax.shard_map(
        run, mesh=mesh, in_specs=in_specs, out_specs=P(None, both, None), check_vma=False
    )
```

```python
import functools
import math

import jax
import jax.numpy as jnp
from jax import lax
from jax.experimental import pallas as pl
from jax.experimental.pallas import tpu as pltpu
from jax.sharding import PartitionSpec as P

MESH = pl.DeviceIdType.MESH
F32 = jnp.float32
BF16 = jnp.bfloat16
NT = (((1,), (1,)), ((), ()))


def dot_nt(a, b):
    return lax.dot_general(a, b, NT, preferred_element_type=F32)


def split3(v):
    hi = v.astype(BF16).astype(F32)
    rest = v - hi
    mid = rest.astype(BF16).astype(F32)
    return hi, mid, rest - mid


def kernel(
    dims,
    ahead,
    pos_hbm,
    den_hbm,
    off_hbm,
    cnt_hbm,
    ids_hbm,
    ops_hbm,
    lat_idx_hbm,
    up_hbm,
    m2l_hbm,
    lat_hbm,
    down_hbm,
    out_ref,
    pos_ref,
    den_ref,
    off_ref,
    cnt_ref,
    ids_ref,
    ops_ref,
    lat_idx_ref,
    up_v,
    m2l_v,
    lat_v,
    down_v,
    halo,
    id_s,
    op_s,
    csend,
    crecv,
    gz,
    stage,
    plane,
    psend,
    precv,
    b_s,
    a_s,
    l_s,
    at_s,
    m_s,
    acc_s,
    wsem,
    zsend,
    zrecv,
    xsend,
    xrecv,
    hsend,
    hrecv,
    osend,
    orecv,
):
    nz, ny, nx = dims
    planes = ny * nx
    per_z = 2 * ny
    leaf = lax.axis_index("leaf")
    rep = lax.axis_index("rep")
    z = leaf // per_z
    y = lax.rem(leaf // 2, ny)
    core = lax.rem(leaf, 2)
    box = leaf * nx + rep
    boxes = nz * ny * nx * 2
    me_p = y * nx + rep

    def z_peer(d):
        return (lax.rem(z + d, nz) * per_z + y * 2 + core, rep)

    def p_peer(d):
        return (
            z * per_z + lax.rem(y + d // nx, ny) * 2 + core,
            lax.rem(rep + lax.rem(d, nx), nx),
        )

    partner = (leaf + 1 - 2 * core, rep)
    after = lax.rem(box + 1, boxes)
    before = lax.rem(box + boxes - 1, boxes)
    after = (after // nx, lax.rem(after, nx))
    before = (before // nx, lax.rem(before, nx))

    loads = [
        pltpu.make_async_copy(src, dst, wsem.at[i])
        for i, (src, dst) in enumerate(
            [
                (pos_hbm, pos_ref),
                (den_hbm, den_ref),
                (up_hbm, up_v),
                (ids_hbm, ids_ref),
                (ops_hbm, ops_ref),
                (off_hbm, off_ref),
                (cnt_hbm, cnt_ref),
                (lat_idx_hbm, lat_idx_ref),
                (m2l_hbm, m2l_v),
                (lat_hbm, lat_v),
                (down_hbm, down_v),
            ]
        )
    ]
    for load in loads[:8]:
        load.start()

    leaves = pos_ref.shape[1]
    barrier = pltpu.get_barrier_semaphore()

    def greet(peer):
        pl.semaphore_signal(barrier, inc=1, device_id=peer, device_id_type=MESH)

    def far_first(k):
        return nz // 2 + ((k + 1) // 2) * (1 - 2 * lax.rem(k, 2))

    @pl.loop(0, nz - 1)
    def _(k):
        greet(z_peer(far_first(k)))

    @pl.loop(1, planes)
    def _(d):
        greet(p_peer(d))

    greet(partner)
    greet(after)
    greet(before)

    for load in loads[:2]:
        load.wait()
    x = [pos_ref[c] for c in range(3)]
    f = [den_ref[c] for c in range(3)]
    x2 = x[0] * x[0] + x[1] * x[1] + x[2] * x[2]
    damping = 1.0 / (1.0 + x2)
    summed = jnp.concatenate(
        [jnp.sum(f[c] * damping, axis=0, keepdims=True) for c in range(3)], axis=1
    )
    summed = jnp.broadcast_to(summed, (8, summed.shape[1])).astype(BF16)
    loads[2].wait()
    coarse = dot_nt(summed, up_v[...]).astype(BF16).astype(F32)
    gz[z] = coarse[0:1]

    def source_rows(lo, sx_, sf_):
        n = sx_[0].shape[0]
        at = pl.ds(lo, n)
        one, zero = jnp.ones(sx_[0].shape, F32), jnp.zeros(sx_[0].shape, F32)
        yy = [v.astype(BF16).astype(F32) for v in sx_]
        ff = [v.astype(BF16).astype(F32) for v in sf_]
        y2 = split3(yy[0] * yy[0] + yy[1] * yy[1] + yy[2] * yy[2])
        yf = split3(-(yy[0] * ff[0] + yy[1] * ff[1] + yy[2] * ff[2]))
        for s in range(3):
            for c in range(3):
                a_s[at, 3 * s + c, 0:128] = -2.0 * yy[c]
                a_s[at, 3 * s + c, 128:256] = ff[c]
            a_s[at, 9 + s, 0:128] = one
            a_s[at, 9 + s, 128:256] = zero
            a_s[at, 12 + s, 0:128] = y2[s]
            a_s[at, 12 + s, 128:256] = yf[s]
            l_s[at, s, 0:128] = ff[s]
            l_s[at, s, 128:256] = -yy[s]
        a_s[at, 15, 0:128] = zero
        a_s[at, 15, 128:256] = zero
        l_s[at, 3, 0:128] = zero
        l_s[at, 3, 128:256] = one
        for r in range(4, 8):
            l_s[at, r, 0:128] = zero
            l_s[at, r, 128:256] = zero

    def turn(lo, hi):
        @pl.loop(lo, hi)
        def _(i):
            at_s[i] = a_s[i].T.astype(BF16)

    def near(lo, hi):
        @pl.loop(lo, hi)
        def _(j):
            g = 2 * j
            pair = [b_s[g].astype(BF16), b_s[g + 1].astype(BF16)]
            both = jnp.concatenate(pair, axis=1)
            totals = [jnp.zeros((8, 128), F32)] * 2
            for o in range(6):
                used_by = [t for t in range(2) if 0 <= o - t < 5]
                target = both if len(used_by) == 2 else pair[used_by[0]]
                qp = jnp.dot(at_s[g + o], target, preferred_element_type=F32)
                inv = lax.rsqrt(qp[0:128])
                w = qp[128:256] * (inv * inv * inv)
                terms = jnp.concatenate([inv, w], axis=0).astype(BF16)
                r = jnp.dot(l_s[g + o].astype(BF16), terms, preferred_element_type=F32)
                for i, t in enumerate(used_by):
                    weight = m_s[o - t, pl.ds(g + t, 1), :]
                    totals[t] = totals[t] + r[:, 128 * i : 128 * (i + 1)] * weight
            acc_s[g] = totals[0]
            acc_s[g + 1] = totals[1]

    def inner():
        for load in loads[5:7]:
            load.wait()
        leaf_rows = lax.broadcasted_iota(jnp.int32, off_ref.shape, 0)
        slots = lax.broadcasted_iota(jnp.int32, off_ref.shape, 1)
        used = jnp.zeros(off_ref.shape, jnp.int32)
        for g in range(leaves):
            used = jnp.where(leaf_rows == g, cnt_ref[g], used)
        for o in range(5):
            hit = jnp.where((off_ref[...] == o - 2) & (slots < used), 1.0, 0.0)
            m_s[o] = jnp.broadcast_to(jnp.sum(hit, axis=1, keepdims=True), x2.shape)

        ones = jnp.ones(x2.shape, F32)
        zeros = jnp.zeros(x2.shape, F32)
        parts = [split3(v) for v in x]
        for s in range(3):
            for c in range(3):
                b_s[:, 3 * s + c, :] = parts[c][s]
        for s, v in enumerate(split3(x2 + 0.05)):
            b_s[:, 9 + s, :] = v
            b_s[:, 12 + s, :] = ones
        b_s[:, 15, :] = zeros
        source_rows(2, x, f)
        turn(2, leaves + 2)
        near(1, leaves // 2 - 1)

    @pl.when(z < ahead)
    def _():
        inner()

    pl.semaphore_wait(barrier, nz + planes + 1)

    def z_copy(d):
        return pltpu.make_async_remote_copy(
            src_ref=gz.at[z],
            dst_ref=gz.at[z],
            send_sem=zsend.at[d],
            recv_sem=zrecv.at[d],
            device_id=z_peer(d),
            device_id_type=MESH,
        )

    def p_copy(part, d):
        return pltpu.make_async_remote_copy(
            src_ref=plane.at[part, me_p],
            dst_ref=plane.at[part, me_p],
            send_sem=xsend.at[part, d],
            recv_sem=xrecv.at[part, d],
            device_id=p_peer(d),
            device_id_type=MESH,
        )

    @pl.loop(0, nz - 1)
    def _(k):
        z_copy(far_first(k)).start()

    def remote(src, dst, s, r, peer):
        return pltpu.make_async_remote_copy(
            src_ref=src, dst_ref=dst, send_sem=s, recv_sem=r, device_id=peer, device_id_type=MESH
        )

    high = pl.ds(leaves - 8, 8)
    halos = [
        remote(pos_ref.at[:, high, :], halo.at[0], hsend.at[0], hrecv.at[0], after),
        remote(den_ref.at[:, high, :], halo.at[1], hsend.at[1], hrecv.at[1], after),
        remote(pos_ref.at[:, 0:8, :], halo.at[2], hsend.at[2], hrecv.at[2], before),
        remote(den_ref.at[:, 0:8, :], halo.at[3], hsend.at[3], hrecv.at[3], before),
    ]
    for copy in halos:
        copy.start()
    for load in loads[8:]:
        load.start()

    for load in loads[3:5]:
        load.wait()
    half = boxes // 2
    group, quarter = nz // 2, nz // 4
    gb = group.bit_length() - 1
    id_s[...] = jnp.full(id_s.shape, -1, jnp.int32)
    op_s[...] = jnp.full(op_s.shape, -1, jnp.int32)
    nil = ids_ref.shape[1]
    id_s[0:1, 0:nil] = ids_ref[...]
    op_s[0:1, 0:nil] = ops_ref[...]
    ids = id_s[0:1, :]
    kinds = op_s[0:1, :]
    sx, sy = nx.bit_length() - 1, ny.bit_length() - 1
    id_x = ids & (nx - 1)
    id_core = (ids >> sx) & 1
    id_y = (ids >> (sx + 1)) & (ny - 1)
    id_z = ids >> (sx + 1 + sy)
    slot = (id_z - z + quarter) & (nz - 1)
    column = (slot >> gb) * (planes * group) + (id_y * nx + id_x) * group + (slot & (group - 1))
    column = jnp.where(ids < 0, -1, id_core * half + column)
    width = ids.shape[1]
    rows = lax.broadcasted_iota(jnp.int32, (boxes, width), 0)
    hot = jnp.where(rows == column, 1.0, 0.0).astype(BF16)
    kind_rows = lax.broadcasted_iota(jnp.int32, (8, width), 0)
    picks = jnp.where(kind_rows == kinds, 1.0, 0.0).astype(BF16)
    counts = dot_nt(picks, hot)
    one_row = lax.broadcasted_iota(jnp.int32, counts.shape, 0) == 4
    counts = jnp.where(one_row, 1.0, counts)
    left, right = counts[:, :half], counts[:, half:]
    first = core == 0
    csend[...] = jnp.where(first, right, left)
    own_counts = jnp.where(first, left, right)
    share = remote(csend, crecv, osend.at[0], orecv.at[0], partner)
    share.start()

    @pl.when(z >= ahead)
    def _():
        inner()


    def hops(d):
        up, along = d // nx, d % nx
        return min(up, ny - up) + min(along, nx - along)

    def forward(part):
        for i in range(group):
            stage[i : i + 1, :] = gz[lax.rem(z + part * group + i - quarter + nz, nz)]
        plane[part, me_p] = stage[...].astype(BF16)

        for d in sorted(range(1, planes), key=hops, reverse=True):
            p_copy(part, d).start()

    def z_wait(lo, hi):
        @pl.loop(lo, hi)
        def _(d):
            z_copy(d).wait_recv()

    z_wait(1, quarter + 1)
    z_wait(nz - quarter + 1, nz)
    forward(0)


    share.wait_recv()
    selector = jnp.concatenate([own_counts, crecv[...]], axis=0).astype(BF16)
    for load in loads[7:]:
        load.wait()

    z_wait(quarter + 1, nz - quarter + 1)
    forward(1)
    for copy in halos:
        copy.wait_recv()
    source_rows(0, [halo[0, c, 6:8, :] for c in range(3)], [halo[1, c, 6:8, :] for c in range(3)])
    source_rows(
        leaves + 2, [halo[2, c, 0:2, :] for c in range(3)], [halo[3, c, 0:2, :] for c in range(3)]
    )
    turn(0, 2)
    turn(leaves + 2, leaves + 4)
    near(0, 1)
    near(leaves // 2 - 1, leaves // 2)

    scale = 1.0 / (8.0 * math.pi)
    lever = acc_s[:, 3, :]
    near_part = [(acc_s[:, c, :] + x[c] * lever) * scale for c in range(3)]

    def gathered(part):
        @pl.loop(1, planes)
        def _(d):
            p_copy(part, d).wait_recv()

        n = planes * group
        blocks = plane[part].reshape(n, plane.shape[3])
        return jnp.dot(selector[:, part * n : (part + 1) * n], blocks, preferred_element_type=F32)

    partial = gathered(0)
    partial = partial + gathered(1)
    psend[...] = partial[8:16]
    swap = remote(psend, precv, osend.at[1], orecv.at[1], partner)
    swap.start()
    swap.wait_recv()
    grouped = (partial[0:8] + precv[...]).astype(BF16)

    def spread(t):
        return jnp.broadcast_to(grouped[t : t + 1].astype(F32), grouped.shape)

    lat_idx = lat_idx_ref[0]
    total = spread(4)
    local = jnp.zeros(grouped.shape, F32)
    for t in range(4):
        local = local + dot_nt(spread(t).astype(BF16), m2l_v[t])
    for i in range(2):
        kept = jnp.where(lat_idx == i, total, 0.0).astype(BF16)
        local = local + dot_nt(kept, lat_v[i])
    far = dot_nt(local.astype(BF16), down_v[...])
    for c in range(3):
        out_ref[c] = near_part[c] + damping * far[0:1, 128 * c : 128 * (c + 1)]

    @pl.loop(1, nz)
    def _(d):
        z_copy(d).wait_send()

    @pl.loop(1, planes)
    def _(d):
        p_copy(0, d).wait_send()
        p_copy(1, d).wait_send()

    for copy in halos + [share, swap]:
        copy.wait_send()


def body(dims, ahead, pos, den, off, cnt, ids, ops, lat_idx, up, m2l, lat, down):
    nz, ny, nx = dims
    planes = ny * nx
    boxes = nz * planes * 2
    leaves = pos.shape[1]
    coef = up.shape[0]
    vm = pl.BlockSpec(memory_space=pltpu.VMEM)
    hbm = pl.BlockSpec(memory_space=pltpu.HBM)
    dma = pltpu.SemaphoreType.DMA
    return pl.pallas_call(
        functools.partial(kernel, dims, ahead),
        out_shape=jax.ShapeDtypeStruct(pos.shape, F32),
        in_specs=[hbm] * 11,
        out_specs=vm,
        scratch_shapes=[
            pltpu.VMEM(pos.shape, F32),
            pltpu.VMEM(den.shape, F32),
            pltpu.VMEM(off.shape, jnp.int32),
            pltpu.SMEM(cnt.shape, jnp.int32),
            pltpu.VMEM(ids.shape, jnp.int32),
            pltpu.VMEM(ops.shape, jnp.int32),
            pltpu.SMEM(lat_idx.shape, jnp.int32),
            pltpu.VMEM(up.shape, BF16),
            pltpu.VMEM(m2l.shape, BF16),
            pltpu.VMEM(lat.shape, BF16),
            pltpu.VMEM(down.shape, BF16),
            pltpu.VMEM((4, 3, 8, 128), F32),
            pltpu.VMEM((8, 256), jnp.int32),
            pltpu.VMEM((8, 256), jnp.int32),
            pltpu.VMEM((8, boxes // 2), F32),
            pltpu.VMEM((8, boxes // 2), F32),
            pltpu.VMEM((nz, 1, coef), F32),
            pltpu.VMEM((nz // 2, coef), F32),
            pltpu.VMEM((2, planes, nz // 2, coef), BF16),
            pltpu.VMEM((8, coef), F32),
            pltpu.VMEM((8, coef), F32),
            pltpu.VMEM((leaves, 16, 128), F32),
            pltpu.VMEM((leaves + 4, 16, 256), F32),
            pltpu.VMEM((leaves + 4, 8, 256), F32),
            pltpu.VMEM((leaves + 4, 256, 16), BF16),
            pltpu.VMEM((5, leaves, 128), F32),
            pltpu.VMEM((leaves, 8, 128), F32),
            dma((11,)),
            dma((nz,)),
            dma((nz,)),
            dma((2, planes)),
            dma((2, planes)),
            dma((4,)),
            dma((4,)),
            dma((2,)),
            dma((2,)),
        ],
        compiler_params=pltpu.CompilerParams(
            collective_id=0, has_side_effects=True, vmem_limit_bytes=67043328
        ),
        name="fmm",
    )(pos, den, off, cnt, ids, ops, lat_idx, up, m2l, lat, down)


def solution(mesh):
    sizes = dict(mesh.shape)
    nx = sizes["rep"]
    ny = 4
    nz = sizes["leaf"] // (2 * ny)
    both = ("leaf", "rep")
    in_specs = (
        P(None, both, None),
        P(None, both, None),
        P(both, None),
        P(both),
        P(both, None),
        P(both, None),
        P(both),
        P(),
        P(),
        P(),
        P(),
    )
    run = functools.partial(body, (nz, ny, nx), nz // 4 + 1)
    return jax.shard_map(
        run, mesh=mesh, in_specs=in_specs, out_specs=P(None, both, None), check_vma=False
    )
```
